128 devices in a mesh: inlet: 4 (over y), row: 32 (over z, x, core).
Axes of the slice: x: 4, y: 4, z: 4, core: 2. Of those that a mesh axis runs over, the one named last changes fastest.
Arguments:
- coeffs: float32 [4, 1024, 1024], P('inlet', 'row'), may hold values from -6 to 6
- basis: float32 [4, 8192, 3, 1024], P('inlet', 'row'), may hold values from -0.1875 to 0.1875
- route: int32 [32768, 1], P(('inlet', 'row')), may hold values from 0 to 127; in each aligned block of 256 rows (0 to 255, 256 to 511, ...) at most 3 rows name the same one
Outputs:
- inflow: bfloat16 [49152, 3, 1024], P(('inlet', 'row'))
The draws below stay inside these ranges and needn't reach their ends.
Inputs may be any that keep to these rules, and one draw needn't show every extreme that they name: `route`: among the rows of one device, no owner is named more than 3 times, a bound that some block reaches.
All inputs are finite; a program needn't handle non-finite values.
Results may differ from the reference program's by a relative error of at most 0.001.
Values may be sent and summed in bfloat16 or wider, within the bound.
No kernel may reach another device: no remote copies, remote signals or barrier semaphores. Data moves between devices by JAX's collectives and lax.ppermute only.
A program may use at most 64 MiB of HBM per device.

```python
import math
import jax
import jax.numpy as jnp
import numpy as np
from jax import lax

MODES = 1024
STEPS = 1024
PTS_DEV = 256
INLETS = 4
PTS_INLET = 8192
CAP = 3
N_INLET = 4
N_ROW = 32


def shard_levels(stream_key, dims, shards, smallest, high):
    def one(position, parts):
        draws = jax.random.uniform(jax.random.fold_in(jax.random.fold_in(stream_key, 6), position), (parts,), jnp.float32, smallest / len(shards), high / len(shards))
        return jnp.repeat(jnp.exp(draws), dims[position] // parts).reshape((-1,) + (1,) * (len(dims) - position - 1))

    factor_of = one(*shards[0])
    for cut in shards[1:]:
        factor_of = factor_of * one(*cut)
    return factor_of


def routed_block(own_key, own, number, rows, number_of, top, reach, lean):
    order = jax.random.permutation(own_key, number_of)
    heavy_load, common = load_shares(number_of, rows * top, reach, lean, True), load_shares(number_of, rows * top, reach, lean, False)
    places = jnp.arange(number_of)

    def named(lengths, rotation):
        used = int((lengths > 0).sum())
        fixed = max(1, used // 4)
        shifted = fixed + (places - fixed + rotation * (used - fixed)) % max(1, number_of - fixed)
        return jnp.zeros((number_of,), jnp.int32).at[order[jnp.where(places < fixed, places, shifted)]].set(jnp.asarray(lengths, jnp.int32))

    lengths = jnp.where(number % 4 == 0, named(heavy_load, number // 4), named(common, number - number // 4 - 1))
    mixed = jax.random.permutation(jax.random.fold_in(own, 3), number_of)
    giver, sink = mixed[0:number_of // 2 * 2:2], mixed[1:number_of // 2 * 2:2]
    room = jnp.minimum(lengths[giver] - 1, reach - lengths[sink]) // 2
    room = jnp.where((giver == order[0]) | (sink == order[0]) | (lengths[sink] == 0), 0, jnp.maximum(room, 0))
    shifted = jax.random.randint(jax.random.fold_in(own, 4), (number_of // 2,), 0, 1 << 20) % (room + 1)
    lengths = lengths.at[giver].add(-shifted).at[sink].add(shifted)
    members = jnp.searchsorted(jnp.cumsum(lengths), jnp.arange(rows * top), side="right").astype(jnp.int32)
    table = members.reshape(top, rows).T
    table = table[jax.random.permutation(jax.random.fold_in(own, 1), rows)]
    rotation = jax.random.randint(jax.random.fold_in(own, 2), (rows, 1), 0, top)
    return jnp.take_along_axis(table, (jnp.arange(top)[None, :] + rotation) % top, axis=1)


def load_shares(amount, total, most, skew, full):
    weights = [(1 << 20) // math.isqrt(standing ** skew) + 1 for standing in range(1, amount + 1)]
    largest = most if full else min(most, max(-(-total // amount), total * weights[0] // sum(weights)))
    least = 1 if total - largest >= amount - 1 else 0
    counts, rest = [largest] + [least] * (amount - 1), total - largest - least * (amount - 1)
    while rest > 0:
        candidates = [i for i in range(1, amount) if counts[i] < largest] or [i for i in range(1, amount) if counts[i] < most]
        pool, budget = sum([weights[i] for i in candidates]), rest
        for i in candidates:
            addition = min(most - counts[i], max(1, budget * weights[i] // pool), rest)
            counts[i] = counts[i] + addition
            rest = rest - addition
    return np.array(counts)


def bell_draw(stream_key, shape, width, reach, split=(), kind=jnp.bfloat16):
    factor_of = shard_levels(stream_key, shape, split, -0.22, 0.18) if split else 1.0
    values = jax.random.normal(stream_key, shape, jnp.float32) * width * factor_of
    return jnp.minimum(jnp.maximum(values, -reach), reach).astype(kind)


def setup_inputs(seed: int = 0) -> dict:
    seeds = jax.random.split(jax.random.key(seed), 4)
    coeffs = bell_draw(seeds[0], (INLETS, STEPS, MODES), 1.0, 6.0, ((0, 4), (1, 32)), jnp.float32)
    basis = bell_draw(seeds[1], (INLETS, PTS_INLET, 3, MODES), MODES ** -0.5, 0.1875, ((0, 4), (1, 32)), jnp.float32)
    route_keys = jax.random.split(jax.random.fold_in(seeds[2], 1), (INLETS * PTS_INLET) // PTS_DEV)
    route_turns = jax.random.permutation(jax.random.fold_in(seeds[2], 3), (INLETS * PTS_INLET) // PTS_DEV)
    route = jax.vmap(lambda own, number: routed_block(jax.random.fold_in(seeds[2], 2), own, number, PTS_DEV, N_INLET * N_ROW, 1, CAP, 2))(route_keys, route_turns).reshape((INLETS * PTS_INLET, 1))
    return {"coeffs": coeffs, "basis": basis, "route": route}


def reference(coeffs, basis, route):
    count = N_INLET * N_ROW
    per_source = basis.reshape(count, PTS_DEV, 3, MODES)
    owners = route.reshape(count, PTS_DEV)
    result = jnp.zeros((count, count, CAP, 3 * STEPS), jnp.bfloat16)

    def place(source, result):
        source = jnp.asarray(source).astype(jnp.int32)
        inlet_index = (source // N_ROW).astype(jnp.int32)
        block = lax.dynamic_index_in_dim(per_source, source, 0, keepdims=False)
        panel = lax.dynamic_index_in_dim(coeffs, inlet_index, 0, keepdims=False)
        velocity = jnp.einsum("pcm,tm->pct", block, panel, precision=lax.Precision.HIGHEST)
        velocity = velocity.astype(jnp.bfloat16).reshape(PTS_DEV, 3 * STEPS)
        owner = lax.dynamic_index_in_dim(owners, source, 0, keepdims=False)
        onehot = (owner[:, None] == jnp.arange(count, dtype=jnp.int32)[None, :]).astype(jnp.int32)
        running = jnp.cumsum(onehot, axis=0)
        rank = jnp.sum(onehot * running, axis=1) - 1
        slot = (owner * CAP + rank).astype(jnp.int32)
        packed = jnp.zeros((count * CAP, 3 * STEPS), jnp.bfloat16).at[slot].set(velocity)
        packed = packed.reshape(count, 1, CAP, 3 * STEPS)
        zero = jnp.int32(0)
        return lax.dynamic_update_slice(result, packed, (zero, source, zero, zero))

    result = lax.fori_loop(0, count, place, result)
    return result.reshape(count * count * CAP, 3, STEPS)
```

```python
import functools

import jax
import jax.numpy as jnp
from jax import lax
from jax.experimental import pallas as pl
from jax.experimental.pallas import tpu as pltpu
from jax.sharding import PartitionSpec as P


SIDE = 4
HOPS = (0, 1, 3, 2)
DEVICES = 128
CAP = 3
COMPS = 3
LANES = 128


def place(z, x, c):
    return (z * SIDE + x) * 2 + c


def turn(array, first, second, k):
    pairs = []
    for z in range(SIDE):
        for x in range(SIDE):
            for c in range(2):
                axis = (first, second)[c]
                tz = (z + k) % SIDE if axis == "z" else z
                tx = (x + k) % SIDE if axis == "x" else x
                pairs.append((place(z, x, c), place(tz, tx, c)))
    return lax.ppermute(array, "row", pairs)


def partner(array):
    return lax.ppermute(array, "row", [(i, i ^ 1) for i in range(2 * SIDE * SIDE)])


def split(value):
    high = value.astype(jnp.bfloat16)
    return high, (value - high.astype(jnp.float32)).astype(jnp.bfloat16)


def build_kernel(points, modes, rows, coord, route, basis, *refs):
    pieces = refs[:8]
    message = refs[8]
    coef, base, base_hi, base_lo, spread, sems = refs[9:]
    z, x, c = coord[0], coord[1], coord[2]
    copies = [pltpu.make_async_copy(basis, base, sems.at[0])]
    for side in range(2):
        core = c if side == 0 else 1 - c
        for outer in range(4):
            for inner in range(4):
                dz = jnp.where(core == 0, HOPS[inner], HOPS[outer])
                dx = jnp.where(core == 0, HOPS[outer], HOPS[inner])
                sz = lax.rem(z - dz + SIDE, SIDE)
                sx = lax.rem(x - dx + SIDE, SIDE)
                start = pl.multiple_of(((sz * SIDE + sx) * 2 + core) * rows, rows)
                copies.append(
                    pltpu.make_async_copy(
                        pieces[side * 4 + outer].at[inner],
                        coef.at[pl.ds(start, rows)],
                        sems.at[len(copies)],
                    )
                )
    for copy in copies:
        copy.start()

    owner = route[...]
    mine = lax.broadcasted_iota(jnp.int32, (DEVICES, points), 0) == owner
    hot = mine.astype(jnp.float32)
    before = lax.broadcasted_iota(jnp.int32, (points, points), 0) < lax.broadcasted_iota(
        jnp.int32, (points, points), 1
    )
    count = jnp.dot(
        hot.astype(jnp.bfloat16),
        before.astype(jnp.float32).astype(jnp.bfloat16),
        preferred_element_type=jnp.float32,
    )
    picks = [
        jnp.where(mine & (count == float(r)), 1.0, 0.0).astype(jnp.bfloat16) for r in range(CAP)
    ]

    copies[0].wait()
    for comp in range(COMPS):
        high, low = split(base[comp])
        base_hi[pl.ds(comp * points, points), :] = high
        base_lo[pl.ds(comp * points, points), :] = low
    for copy in copies[1:]:
        copy.wait()

    width = 2 * LANES
    contract = functools.partial(
        lax.dot_general,
        dimension_numbers=(((1,), (1,)), ((), ())),
        preferred_element_type=jnp.float32,
    )

    def step(i, _):
        high, low = split(coef[pl.ds(pl.multiple_of(i * width, width), width), :])
        value = contract(base_hi[...], low)
        value = value + contract(base_lo[...], high)
        value = value + contract(base_hi[...], high)
        value = value.astype(jnp.bfloat16)
        for comp in range(COMPS):
            block = value[comp * points : (comp + 1) * points, :]
            for r in range(CAP):
                moved = jnp.dot(picks[r], block, preferred_element_type=jnp.float32)
                for half in range(2):
                    spread[r * COMPS + comp, pl.ds(i * 2 + half, DEVICES, stride=8), :] = moved[
                        :, half * LANES : (half + 1) * LANES
                    ]
        return 0

    lax.fori_loop(0, coef.shape[0] // width, step, 0)
    for row in range(CAP * COMPS):
        message[:, pl.ds(row * 8, 8), :] = (
            spread[row].reshape(DEVICES, 8, LANES).astype(jnp.bfloat16)
        )


def build(coord, route, basis, pieces):
    comps, points, modes = basis.shape
    rows = pieces[0].shape[1]
    steps = 32 * rows
    anywhere = pl.BlockSpec(memory_space=pl.ANY)
    whole = pl.BlockSpec(memory_space=pltpu.VMEM)
    return pl.pallas_call(
        functools.partial(build_kernel, points, modes, rows),
        out_shape=jax.ShapeDtypeStruct((DEVICES, CAP * COMPS * 8, LANES), jnp.bfloat16),
        in_specs=[pl.BlockSpec(memory_space=pltpu.SMEM), whole, anywhere] + [anywhere] * 8,
        out_specs=whole,
        scratch_shapes=[
            pltpu.VMEM((steps, modes), jnp.float32),
            pltpu.VMEM((comps, points, modes), jnp.float32),
            pltpu.VMEM((comps * points, modes), jnp.bfloat16),
            pltpu.VMEM((comps * points, modes), jnp.bfloat16),
            pltpu.VMEM((CAP * COMPS, DEVICES * 8, LANES), jnp.float32),
            pltpu.SemaphoreType.DMA((33,)),
        ],
        name="build",
    )(coord, route, basis, *pieces)


def settle_kernel(count, received, out, wide, narrow):
    wide[...] = received[...].reshape(count * 72, LANES).astype(jnp.float32)
    for comp in range(COMPS):
        for j in range(8):
            for r in range(CAP):
                narrow[pl.ds(r, count, stride=CAP), :] = wide[
                    pl.ds((r * COMPS + comp) * 8 + j, count, stride=72), :
                ]
            out[comp, :, pl.ds(j * LANES, LANES)] = narrow[...].astype(jnp.bfloat16)


def settle(received):
    count = 16
    return pl.pallas_call(
        functools.partial(settle_kernel, count),
        grid=(DEVICES // count,),
        out_shape=jax.ShapeDtypeStruct((COMPS, DEVICES * CAP, 8 * LANES), jnp.bfloat16),
        in_specs=[pl.BlockSpec((count, 72, LANES), lambda i: (i, 0, 0))],
        out_specs=pl.BlockSpec((COMPS, count * CAP, 8 * LANES), lambda i: (0, i, 0)),
        scratch_shapes=[
            pltpu.VMEM((count * 72, LANES), jnp.float32),
            pltpu.VMEM((count * CAP, LANES), jnp.float32),
        ],
        name="settle",
    )(received)


def local(coeffs, basis, route):
    own = coeffs[0]
    line = jnp.stack([own] + [turn(own, "z", "x", k) for k in HOPS[1:]])
    plane = [line] + [turn(line, "x", "z", k) for k in HOPS[1:]]
    other = [partner(piece) for piece in plane]
    row = lax.axis_index("row")
    coord = jnp.stack([row // 8, row // 2 % 4, row % 2]).astype(jnp.int32)
    message = build(coord, route.reshape(1, -1), jnp.transpose(basis[0], (1, 0, 2)), plane + other)
    received = lax.all_to_all(message, ("inlet", "row"), split_axis=0, concat_axis=0, tiled=True)
    return jnp.transpose(settle(received), (1, 0, 2))


def solution(mesh):
    in_specs = (P("inlet", "row", None), P("inlet", "row", None, None), P(("inlet", "row"), None))
    out_specs = P(("inlet", "row"), None, None)
    return jax.shard_map(local, mesh=mesh, in_specs=in_specs, out_specs=out_specs, check_vma=False)
```

```python
import functools

import jax
import jax.numpy as jnp
from jax import lax
from jax.experimental import pallas as pl
from jax.experimental.pallas import tpu as pltpu
from jax.sharding import PartitionSpec as P


SIDE = 4
HOPS = (0, 1, 3, 2)
DEVICES = 128
CAP = 3
COMPS = 3
LANES = 128


def place(z, x, c):
    return (z * SIDE + x) * 2 + c


def turn(array, first, second, k):
    pairs = []
    for z in range(SIDE):
        for x in range(SIDE):
            for c in range(2):
                axis = (first, second)[c]
                tz = (z + k) % SIDE if axis == "z" else z
                tx = (x + k) % SIDE if axis == "x" else x
                pairs.append((place(z, x, c), place(tz, tx, c)))
    return lax.ppermute(array, "row", pairs)


def partner(array):
    return lax.ppermute(array, "row", [(i, i ^ 1) for i in range(2 * SIDE * SIDE)])


def split(value):
    high = value.astype(jnp.bfloat16)
    return high, (value - high.astype(jnp.float32)).astype(jnp.bfloat16)


def prepare_kernel(points, route, basis, high, low, picks, base, sems):
    copies = [
        pltpu.make_async_copy(basis.at[comp], base.at[comp], sems.at[comp]) for comp in range(COMPS)
    ]
    for copy in copies:
        copy.start()
    mine = lax.broadcasted_iota(jnp.int32, (DEVICES, points), 0) == route[...]
    before = lax.broadcasted_iota(jnp.int32, (points, points), 0) < lax.broadcasted_iota(
        jnp.int32, (points, points), 1
    )
    count = jnp.dot(
        jnp.where(mine, 1.0, 0.0).astype(jnp.bfloat16),
        jnp.where(before, 1.0, 0.0).astype(jnp.bfloat16),
        preferred_element_type=jnp.float32,
    )
    for r in range(CAP):
        picks[pl.ds(r * DEVICES, DEVICES), :] = jnp.where(
            mine & (count == float(r)), 1.0, 0.0
        ).astype(jnp.bfloat16)
    for comp in range(COMPS):
        copies[comp].wait()
        high[pl.ds(comp * points, points), :], low[pl.ds(comp * points, points), :] = split(
            base[comp]
        )


def prepare(route, basis):
    comps, points, modes = basis.shape
    whole = pl.BlockSpec(memory_space=pltpu.VMEM)
    half = jax.ShapeDtypeStruct((comps * points, modes), jnp.bfloat16)
    return pl.pallas_call(
        functools.partial(prepare_kernel, points),
        out_shape=(half, half, jax.ShapeDtypeStruct((CAP * DEVICES, points), jnp.bfloat16)),
        in_specs=[whole, pl.BlockSpec(memory_space=pl.ANY)],
        out_specs=(whole, whole, whole),
        scratch_shapes=[
            pltpu.VMEM((comps, points, modes), jnp.float32),
            pltpu.SemaphoreType.DMA((comps,)),
        ],
        compiler_params=pltpu.CompilerParams(vmem_limit_bytes=12 << 20),
        cost_estimate=pl.CostEstimate(flops=20_000_000, bytes_accessed=8 << 20, transcendentals=0),
        name="prepare",
    )(route, basis)


def build_kernel(layout, rows, coord, *refs):
    pieces = refs[: len(layout)]
    high_in, low_in, picks_in, message = refs[len(layout) : len(layout) + 4]
    coef, high, low, picks, spread, packed, base_sems, sems, out_sems = refs[len(layout) + 4 :]
    z, x, c = coord[0], coord[1], coord[2]
    fixed = [
        pltpu.make_async_copy(source, target, base_sems.at[i])
        for i, (source, target) in enumerate(((high_in, high), (low_in, low), (picks_in, picks)))
    ]
    fixed[0].start()
    for piece, (side, outer, inners) in zip(pieces, layout):
        core = c if side == 0 else 1 - c
        for i, inner in enumerate(inners):
            dz = jnp.where(core == 0, inner, outer)
            dx = jnp.where(core == 0, outer, inner)
            sz = lax.rem(z - dz + SIDE, SIDE)
            sx = lax.rem(x - dx + SIDE, SIDE)
            start = pl.multiple_of(((sz * SIDE + sx) * 2 + core) * rows, rows)
            pltpu.make_async_copy(
                piece.at[i], coef.at[pl.ds(start, rows)], sems.at[sz]
            ).start()
    fixed[1].start()
    fixed[2].start()

    points = picks.shape[1]
    width = 8 * rows
    blocks = width // LANES
    contract = functools.partial(
        lax.dot_general,
        dimension_numbers=(((1,), (1,)), ((), ())),
        preferred_element_type=jnp.float32,
    )
    for copy in fixed:
        copy.wait()

    def step(i, _):
        here = coef.at[pl.ds(pl.multiple_of(i * width, width), width)]
        pltpu.make_async_copy(here, here, sems.at[i]).wait()
        top, rest = split(here[...])
        value = contract(high[...], rest)
        value = value + contract(low[...], top)
        value = value + contract(high[...], top)
        value = value.astype(jnp.bfloat16)
        for comp in range(COMPS):
            moved = jnp.dot(
                picks[...],
                value[comp * points : (comp + 1) * points, :],
                preferred_element_type=jnp.float32,
            )
            for r in range(CAP):
                for half in range(blocks):
                    spread[r * COMPS + comp, pl.ds(i * blocks + half, DEVICES, stride=8), :] = (
                        moved[
                            r * DEVICES : (r + 1) * DEVICES, half * LANES : (half + 1) * LANES
                        ]
                    )
        return 0

    lax.fori_loop(0, SIDE, step, 0)
    part = DEVICES // 8

    def leave(i):
        some = pl.ds(i * part, part)
        return pltpu.make_async_copy(packed.at[some], message.at[some], out_sems.at[i])

    def pack(i, _):
        for row in range(CAP * COMPS):
            packed[pl.ds(i * part, part), pl.ds(row * 8, 8), :] = (
                spread[row, pl.ds(pl.multiple_of(i * part * 8, part * 8), part * 8), :]
                .reshape(part, 8, LANES)
                .astype(jnp.bfloat16)
            )
        leave(i).start()
        return 0

    lax.fori_loop(0, 8, pack, 0)
    for i in range(8):
        leave(i).wait()


def build(coord, pieces, layout, high, low, picks):
    rows, modes = pieces[0].shape[1:]
    anywhere = pl.BlockSpec(memory_space=pl.ANY)
    sent = (DEVICES, CAP * COMPS * 8, LANES)
    return pl.pallas_call(
        functools.partial(build_kernel, layout, rows),
        out_shape=jax.ShapeDtypeStruct(sent, jnp.bfloat16),
        in_specs=[pl.BlockSpec(memory_space=pltpu.SMEM)] + [anywhere] * (len(pieces) + 3),
        out_specs=anywhere,
        scratch_shapes=[
            pltpu.VMEM((32 * rows, modes), jnp.float32),
            pltpu.VMEM(high.shape, jnp.bfloat16),
            pltpu.VMEM(low.shape, jnp.bfloat16),
            pltpu.VMEM(picks.shape, jnp.bfloat16),
            pltpu.VMEM((CAP * COMPS, DEVICES * 8, LANES), jnp.float32),
            pltpu.VMEM(sent, jnp.bfloat16),
            pltpu.SemaphoreType.DMA((3,)),
            pltpu.SemaphoreType.DMA((SIDE,)),
            pltpu.SemaphoreType.DMA((8,)),
        ],
        compiler_params=pltpu.CompilerParams(vmem_limit_bytes=32 << 20),
        name="build",
    )(coord, *pieces, high, low, picks)


def settle_kernel(count, received, out, arrived, wide, narrow, ready, in_sems, out_sems):
    parts = DEVICES // count

    def enter(i):
        some = pl.ds(i * count, count)
        return pltpu.make_async_copy(received.at[some], arrived.at[some], in_sems.at[i])

    def lines(i):
        return pl.ds(pl.multiple_of(i * count * CAP, count * CAP), count * CAP)

    def leave(i):
        return pltpu.make_async_copy(ready.at[:, lines(i)], out.at[:, lines(i)], out_sems.at[i])

    for i in range(parts):
        enter(i).start()

    def step(i, _):
        enter(i).wait()
        wide[...] = (
            arrived[pl.ds(i * count, count)].reshape(count * 72, LANES).astype(jnp.float32)
        )
        for comp in range(COMPS):
            for j in range(8):
                for r in range(CAP):
                    narrow[comp * 8 + j, pl.ds(r, count, stride=CAP), :] = wide[
                        pl.ds((r * COMPS + comp) * 8 + j, count, stride=72), :
                    ]
        for comp in range(COMPS):
            for j in range(8):
                ready[comp, lines(i), j * LANES : (j + 1) * LANES] = narrow[comp * 8 + j].astype(
                    jnp.bfloat16
                )
        leave(i).start()
        return 0

    lax.fori_loop(0, parts, step, 0)
    for i in range(parts):
        leave(i).wait()


def settle(received):
    count = 16
    anywhere = pl.BlockSpec(memory_space=pl.ANY)
    shape = (COMPS, DEVICES * CAP, 8 * LANES)
    return pl.pallas_call(
        functools.partial(settle_kernel, count),
        out_shape=jax.ShapeDtypeStruct(shape, jnp.bfloat16),
        in_specs=[anywhere],
        out_specs=anywhere,
        scratch_shapes=[
            pltpu.VMEM(received.shape, jnp.bfloat16),
            pltpu.VMEM((count * 72, LANES), jnp.float32),
            pltpu.VMEM((COMPS * 8, count * CAP, LANES), jnp.float32),
            pltpu.VMEM(shape, jnp.bfloat16),
            pltpu.SemaphoreType.DMA((DEVICES // count,)),
            pltpu.SemaphoreType.DMA((DEVICES // count,)),
        ],
        compiler_params=pltpu.CompilerParams(vmem_limit_bytes=24 << 20),
        name="settle",
    )(received)


def steps(coeffs, basis, route):
    high, low, picks = prepare(route.reshape(1, -1), jnp.transpose(basis[0], (1, 0, 2)))
    own = coeffs[0]
    near = [own]
    for k in HOPS[1:]:
        near.append(turn(own, "z", "x", k))
    line = jnp.stack(near)
    mate = partner(line)
    pieces, layout = [line, mate], [(0, 0, HOPS), (1, 0, HOPS)]

    def far(array, first, second, k, side, inners):
        moved = turn(array, first, second, k)
        pieces.extend([moved, partner(moved)])
        layout.extend([(side, k, inners), (1 - side, k, inners)])

    far(line, "x", "z", 1, 0, HOPS)
    far(line, "x", "z", 3, 0, HOPS)
    far(line[:2], "x", "z", 2, 0, HOPS[:2])
    far(mate[2:], "z", "x", 2, 1, HOPS[2:])
    row = lax.axis_index("row")
    coord = jnp.stack([row // 8, row // 2 % 4, row % 2]).astype(jnp.int32)
    message = build(coord, pieces, tuple(layout), high, low, picks)
    received = lax.all_to_all(message, ("inlet", "row"), split_axis=0, concat_axis=0, tiled=True)
    return jnp.transpose(settle(received), (1, 0, 2))


def solution(mesh):
    in_specs = (P("inlet", "row", None), P("inlet", "row", None, None), P(("inlet", "row"), None))
    out_specs = P(("inlet", "row"), None, None)
    return jax.shard_map(steps, mesh=mesh, in_specs=in_specs, out_specs=out_specs, check_vma=False)
```

```python
import functools

import jax
import jax.numpy as jnp
from jax import lax
from jax.experimental import pallas as pl
from jax.experimental.pallas import tpu as pltpu
from jax.sharding import PartitionSpec as P


SIDE = 4
DEVICES = 128
CAP = 3
COMPS = 3
LANES = 128


def place(z, x, c):
    return (z * SIDE + x) * 2 + c


def turn(array, first, second, k):
    pairs = []
    for z in range(SIDE):
        for x in range(SIDE):
            for c in range(2):
                axis = (first, second)[c]
                tz = (z + k) % SIDE if axis == "z" else z
                tx = (x + k) % SIDE if axis == "x" else x
                pairs.append((place(z, x, c), place(tz, tx, c)))
    return lax.ppermute(array, "row", pairs)


def partner(array):
    return lax.ppermute(array, "row", [(i, i ^ 1) for i in range(2 * SIDE * SIDE)])


def split(value):
    high = value.astype(jnp.bfloat16)
    return high, (value - high.astype(jnp.float32)).astype(jnp.bfloat16)


def prepare_kernel(points, route, basis, high, low, picks_out, base, picks, sems, sem):
    copies = [
        pltpu.make_async_copy(basis.at[comp], base.at[comp], sems.at[comp]) for comp in range(COMPS)
    ]
    for copy in copies:
        copy.start()
    mine = lax.broadcasted_iota(jnp.int32, (DEVICES, points), 0) == route[...]
    before = lax.broadcasted_iota(jnp.int32, (points, points), 0) < lax.broadcasted_iota(
        jnp.int32, (points, points), 1
    )
    count = jnp.dot(
        jnp.where(mine, 1.0, 0.0).astype(jnp.bfloat16),
        jnp.where(before, 1.0, 0.0).astype(jnp.bfloat16),
        preferred_element_type=jnp.float32,
    )
    for r in range(CAP):
        picks[pl.ds(r * DEVICES, DEVICES), :] = jnp.where(
            mine & (count == float(r)), 1.0, 0.0
        ).astype(jnp.bfloat16)
    copy = pltpu.make_async_copy(picks, picks_out, sem)
    copy.start()
    for comp in range(COMPS):
        copies[comp].wait()
        high[pl.ds(comp * points, points), :], low[pl.ds(comp * points, points), :] = split(
            base[comp]
        )
    copy.wait()


def prepare(route, basis):
    comps, points, modes = basis.shape
    whole = pl.BlockSpec(memory_space=pltpu.VMEM)
    half = jax.ShapeDtypeStruct((comps * points, modes), jnp.bfloat16)
    return pl.pallas_call(
        functools.partial(prepare_kernel, points),
        out_shape=(half, half, jax.ShapeDtypeStruct((CAP * DEVICES, points), jnp.bfloat16)),
        in_specs=[whole, pl.BlockSpec(memory_space=pltpu.HBM)],
        out_specs=(whole, whole, pl.BlockSpec(memory_space=pltpu.HBM)),
        scratch_shapes=[
            pltpu.VMEM((comps, points, modes), jnp.float32),
            pltpu.VMEM((CAP * DEVICES, points), jnp.bfloat16),
            pltpu.SemaphoreType.DMA((comps,)),
            pltpu.SemaphoreType.DMA,
        ],
        compiler_params=pltpu.CompilerParams(vmem_limit_bytes=10 << 20),
        cost_estimate=pl.CostEstimate(flops=20_000_000, bytes_accessed=8 << 20, transcendentals=0),
        name="prepare",
    )(route, basis)


def product(points, coef, high, low, result):
    contract = functools.partial(
        lax.dot_general,
        dimension_numbers=(((1,), (1,)), ((), ())),
        preferred_element_type=jnp.float32,
    )
    top, rest = split(coef)
    for comp in range(COMPS):
        there = pl.ds(comp * points, points)
        value = contract(rest, high[there, :])
        value = value + contract(top, low[there, :])
        value = value + contract(top, high[there, :])
        value = value.astype(jnp.bfloat16)
        result[:, :, comp * points : (comp + 1) * points] = value.reshape(
            result.shape[:2] + (points,)
        )


def gathered(pieces):
    modes = pieces[0].shape[-1]
    return jnp.concatenate([piece[...].reshape(-1, modes) for piece in pieces], axis=0)


def expand_kernel(points, high, low, mine, mate, out, result, sem):
    product(points, gathered((mine, mate)), high, low, result)
    copy = pltpu.make_async_copy(result, out, sem)
    copy.start()
    copy.wait()


def expand(mine, mate, high, low, points):
    rows = mine.shape[1]
    shape = (8, rows, COMPS * points)
    return pl.pallas_call(
        functools.partial(expand_kernel, points),
        out_shape=jax.ShapeDtypeStruct(shape, jnp.bfloat16),
        in_specs=[pl.BlockSpec(memory_space=pltpu.VMEM)] * 4,
        out_specs=pl.BlockSpec(memory_space=pltpu.HBM),
        scratch_shapes=[pltpu.VMEM(shape, jnp.bfloat16), pltpu.SemaphoreType.DMA],
        compiler_params=pltpu.CompilerParams(vmem_limit_bytes=10 << 20),
        cost_estimate=pl.CostEstimate(
            flops=1_200_000_000, bytes_accessed=1 << 20, transcendentals=0
        ),
        name="expand",
    )(high, low, mine, mate)


def build_kernel(points, rows, *refs):
    lines, pieces = refs[:3], refs[3:7]
    high, low, picks_in, message = refs[7:11]
    table, picks, chunk, spread, in_sems = refs[11:]
    row = lax.axis_index("row")
    z = row // (2 * SIDE)
    x = lax.rem(row // 2, SIDE)
    c = lax.rem(row, 2)
    copies = [
        pltpu.make_async_copy(line, table.at[k], in_sems.at[i])
        for i, (line, k) in enumerate(zip(lines, (0, 1, 3)))
    ]
    copies.append(pltpu.make_async_copy(picks_in, picks, in_sems.at[3]))
    for copy in copies:
        copy.start()
    product(points, gathered(pieces), high, low, table.at[2])
    for copy in copies:
        copy.wait()

    width = 8 * rows
    blocks = width // LANES

    def step(i, _):
        dz = lax.rem(z - i + SIDE, SIDE)
        for column in range(SIDE):
            dx = lax.rem(x - column + SIDE, SIDE)
            for core in range(2):
                k, inner = (dx, dz) if core == 0 else (dz, dx)
                side = jnp.where(c == core, 0, SIDE)
                chunk[pl.ds((column * 2 + core) * rows, rows), :] = table[k, side + inner]
        for comp in range(COMPS):
            moved = lax.dot_general(
                picks[...],
                chunk[:, comp * points : (comp + 1) * points],
                (((1,), (1,)), ((), ())),
                preferred_element_type=jnp.float32,
            )
            for r in range(CAP):
                for half in range(blocks):
                    spread[r * COMPS + comp, pl.ds(i * blocks + half, DEVICES, stride=8), :] = (
                        moved[
                            r * DEVICES : (r + 1) * DEVICES, half * LANES : (half + 1) * LANES
                        ]
                    )
        return 0

    lax.fori_loop(0, SIDE, step, 0)
    part = DEVICES // 8

    def pack(i, _):
        for row in range(CAP * COMPS):
            message[pl.ds(i * part, part), pl.ds(row * 8, 8), :] = (
                spread[row, pl.ds(pl.multiple_of(i * part * 8, part * 8), part * 8), :]
                .reshape(part, 8, LANES)
                .astype(jnp.bfloat16)
            )
        return 0

    lax.fori_loop(0, 8, pack, 0)


def build(lines, pieces, high, low, picks):
    rows, wide = lines[0].shape[1:]
    points = picks.shape[1]
    remote = pl.BlockSpec(memory_space=pltpu.HBM)
    whole = pl.BlockSpec(memory_space=pltpu.VMEM)
    sent = (DEVICES, CAP * COMPS * 8, LANES)
    return pl.pallas_call(
        functools.partial(build_kernel, points, rows),
        out_shape=jax.ShapeDtypeStruct(sent, jnp.bfloat16),
        in_specs=[remote] * 3 + [whole] * 6 + [remote],
        out_specs=whole,
        scratch_shapes=[
            pltpu.VMEM((SIDE, 8, rows, wide), jnp.bfloat16),
            pltpu.VMEM(picks.shape, jnp.bfloat16),
            pltpu.VMEM((8 * rows, wide), jnp.bfloat16),
            pltpu.VMEM((CAP * COMPS, DEVICES * 8, LANES), jnp.float32),
            pltpu.SemaphoreType.DMA((4,)),
        ],
        compiler_params=pltpu.CompilerParams(vmem_limit_bytes=20 << 20),
        name="build",
    )(*lines, *pieces, high, low, picks)


def settle_kernel(count, received, out, wide, narrow, ready, out_sems):
    parts = DEVICES // count

    def lines(i):
        return pl.ds(pl.multiple_of(i * count * CAP, count * CAP), count * CAP)

    def leave(i):
        return pltpu.make_async_copy(ready.at[:, lines(i)], out.at[:, lines(i)], out_sems.at[i])

    def step(i, _):
        wide[...] = (
            received[pl.ds(i * count, count)].reshape(count * 72, LANES).astype(jnp.float32)
        )
        for comp in range(COMPS):
            for j in range(8):
                for r in range(CAP):
                    narrow[comp * 8 + j, pl.ds(r, count, stride=CAP), :] = wide[
                        pl.ds((r * COMPS + comp) * 8 + j, count, stride=72), :
                    ]
        for comp in range(COMPS):
            for j in range(8):
                ready[comp, lines(i), j * LANES : (j + 1) * LANES] = narrow[comp * 8 + j].astype(
                    jnp.bfloat16
                )
        leave(i).start()
        return 0

    lax.fori_loop(0, parts, step, 0)
    for i in range(parts):
        leave(i).wait()


def settle(received):
    count = 16
    shape = (COMPS, DEVICES * CAP, 8 * LANES)
    return pl.pallas_call(
        functools.partial(settle_kernel, count),
        out_shape=jax.ShapeDtypeStruct(shape, jnp.bfloat16),
        in_specs=[pl.BlockSpec(memory_space=pltpu.VMEM)],
        out_specs=pl.BlockSpec(memory_space=pl.ANY),
        scratch_shapes=[
            pltpu.VMEM((count * 72, LANES), jnp.float32),
            pltpu.VMEM((COMPS * 8, count * CAP, LANES), jnp.float32),
            pltpu.VMEM(shape, jnp.bfloat16),
            pltpu.SemaphoreType.DMA((DEVICES // count,)),
        ],
        compiler_params=pltpu.CompilerParams(vmem_limit_bytes=9 << 20),
        name="settle",
    )(received)


def steps(coeffs, basis, route):
    points = basis.shape[1]
    high, low, picks = prepare(route.reshape(1, -1), jnp.transpose(basis[0], (1, 0, 2)))
    own = coeffs[0]
    near = [own]
    for k in range(1, SIDE):
        near.append(turn(own, "z", "x", k))
    line = jnp.stack(near)
    mate = partner(line)

    def far(array, first, second, k):
        moved = turn(array, first, second, k)
        return moved, partner(moved)

    lines = []
    lines.append(expand(line, mate, high, low, points))
    for k in (1, 3):
        moved, swapped = far(line, "x", "z", k)
        lines.append(expand(moved, swapped, high, low, points))
    a, a_swapped = far(line[:2], "x", "z", 2)
    b, b_swapped = far(mate[2:], "z", "x", 2)
    message = build(lines, (a, b_swapped, a_swapped, b), high, low, picks)
    received = lax.all_to_all(message, ("inlet", "row"), split_axis=0, concat_axis=0, tiled=True)
    return jnp.transpose(settle(received), (1, 0, 2))


def solution(mesh):
    in_specs = (P("inlet", "row", None), P("inlet", "row", None, None), P(("inlet", "row"), None))
    out_specs = P(("inlet", "row"), None, None)
    return jax.shard_map(steps, mesh=mesh, in_specs=in_specs, out_specs=out_specs, check_vma=False)
```

```python
import functools

import jax
import jax.numpy as jnp
from jax import lax
from jax.experimental import pallas as pl
from jax.experimental.pallas import tpu as pltpu
from jax.sharding import Mesh
from jax.sharding import PartitionSpec as P


SIDE = 4
DEVICES = 128
CAP = 3
COMPS = 3
LANES = 128


def place(z, x, c):
    return (z * SIDE + x) * 2 + c


def position(y, z, x, c):
    return ((c * SIDE + z) * SIDE + y) * SIDE + x


def device_at(slot):
    y, z, x, c = (slot >> 2) & 3, (slot >> 4) & 3, slot & 3, slot >> 6
    return ((y * SIDE + z) * SIDE + x) * 2 + c


def turn(array, first, second, k):
    pairs = []
    for z in range(SIDE):
        for x in range(SIDE):
            for c in range(2):
                axis = (first, second)[c]
                tz = (z + k) % SIDE if axis == "z" else z
                tx = (x + k) % SIDE if axis == "x" else x
                pairs.append((place(z, x, c), place(tz, tx, c)))
    return lax.ppermute(array, ("z", "x", "c"), pairs)


def partner(array):
    return lax.ppermute(array, ("z", "x", "c"), [(i, i ^ 1) for i in range(2 * SIDE * SIDE)])


def split(value):
    high = value.astype(jnp.bfloat16)
    return high, (value - high.astype(jnp.float32)).astype(jnp.bfloat16)


def prepare_kernel(points, route, basis, high, low, picks_out, base, picks, sems, sem):
    copies = [
        pltpu.make_async_copy(basis.at[comp], base.at[comp], sems.at[comp]) for comp in range(COMPS)
    ]
    for copy in copies:
        copy.start()
    mine = device_at(lax.broadcasted_iota(jnp.int32, (DEVICES, points), 0)) == route[...]
    before = lax.broadcasted_iota(jnp.int32, (points, points), 0) < lax.broadcasted_iota(
        jnp.int32, (points, points), 1
    )
    count = jnp.dot(
        jnp.where(mine, 1.0, 0.0).astype(jnp.bfloat16),
        jnp.where(before, 1.0, 0.0).astype(jnp.bfloat16),
        preferred_element_type=jnp.float32,
    )
    for r in range(CAP):
        picks[pl.ds(r * DEVICES, DEVICES), :] = jnp.where(
            mine & (count == float(r)), 1.0, 0.0
        ).astype(jnp.bfloat16)
    copy = pltpu.make_async_copy(picks, picks_out, sem)
    copy.start()
    for comp in range(COMPS):
        copies[comp].wait()
        high[pl.ds(comp * points, points), :], low[pl.ds(comp * points, points), :] = split(
            base[comp]
        )
    copy.wait()


def prepare(route, basis):
    comps, points, modes = basis.shape
    whole = pl.BlockSpec(memory_space=pltpu.VMEM)
    half = jax.ShapeDtypeStruct((comps * points, modes), jnp.bfloat16)
    return pl.pallas_call(
        functools.partial(prepare_kernel, points),
        out_shape=(half, half, jax.ShapeDtypeStruct((CAP * DEVICES, points), jnp.bfloat16)),
        in_specs=[whole, pl.BlockSpec(memory_space=pltpu.HBM)],
        out_specs=(whole, whole, pl.BlockSpec(memory_space=pltpu.HBM)),
        scratch_shapes=[
            pltpu.VMEM((comps, points, modes), jnp.float32),
            pltpu.VMEM((CAP * DEVICES, points), jnp.bfloat16),
            pltpu.SemaphoreType.DMA((comps,)),
            pltpu.SemaphoreType.DMA,
        ],
        compiler_params=pltpu.CompilerParams(vmem_limit_bytes=52_000_000),
        cost_estimate=pl.CostEstimate(flops=20_000_000, bytes_accessed=8 << 20, transcendentals=0),
        name="prepare",
    )(route, basis)


def product(points, coef, high, low, result):
    contract = functools.partial(
        lax.dot_general,
        dimension_numbers=(((1,), (1,)), ((), ())),
        preferred_element_type=jnp.float32,
    )
    top, rest = split(coef)
    for comp in range(COMPS):
        there = pl.ds(comp * points, points)
        value = contract(rest, high[there, :])
        value = value + contract(top, low[there, :])
        value = value + contract(top, high[there, :])
        value = value.astype(jnp.bfloat16)
        result[:, :, comp * points : (comp + 1) * points] = value.reshape(
            result.shape[:2] + (points,)
        )


def gathered(pieces):
    modes = pieces[0].shape[-1]
    return jnp.concatenate([piece[...].reshape(-1, modes) for piece in pieces], axis=0)


def expand_kernel(points, high, low, mine, mate, out, result, sem):
    product(points, gathered((mine, mate)), high, low, result)
    copy = pltpu.make_async_copy(result, out, sem)
    copy.start()
    copy.wait()


def expand(mine, mate, high, low, points):
    rows = mine.shape[1]
    shape = (8, rows, COMPS * points)
    return pl.pallas_call(
        functools.partial(expand_kernel, points),
        out_shape=jax.ShapeDtypeStruct(shape, jnp.bfloat16),
        in_specs=[pl.BlockSpec(memory_space=pltpu.VMEM)] * 4,
        out_specs=pl.BlockSpec(memory_space=pltpu.HBM),
        scratch_shapes=[pltpu.VMEM(shape, jnp.bfloat16), pltpu.SemaphoreType.DMA],
        compiler_params=pltpu.CompilerParams(vmem_limit_bytes=10 << 20),
        cost_estimate=pl.CostEstimate(
            flops=1_200_000_000, bytes_accessed=1 << 20, transcendentals=0
        ),
        name="expand",
    )(high, low, mine, mate)


def build_kernel(points, rows, *refs):
    lines, pieces = refs[:3], refs[3:7]
    high, low, picks_in, message = refs[7:11]
    table, picks, chunk, spread, in_sems = refs[11:]
    z, x, c = lax.axis_index("z"), lax.axis_index("x"), lax.axis_index("c")
    copies = [
        pltpu.make_async_copy(line, table.at[k], in_sems.at[i])
        for i, (line, k) in enumerate(zip(lines, (0, 1, 3)))
    ]
    copies.append(pltpu.make_async_copy(picks_in, picks, in_sems.at[3]))
    for copy in copies:
        copy.start()
    product(points, gathered(pieces), high, low, table.at[2])
    for copy in copies:
        copy.wait()

    width = 8 * rows
    blocks = width // LANES

    def step(i, _):
        dz = lax.rem(z - i + SIDE, SIDE)
        for column in range(SIDE):
            dx = lax.rem(x - column + SIDE, SIDE)
            for core in range(2):
                k, inner = (dx, dz) if core == 0 else (dz, dx)
                side = jnp.where(c == core, 0, SIDE)
                chunk[pl.ds((column * 2 + core) * rows, rows), :] = table[k, side + inner]
        for comp in range(COMPS):
            moved = lax.dot_general(
                picks[...],
                chunk[:, comp * points : (comp + 1) * points],
                (((1,), (1,)), ((), ())),
                preferred_element_type=jnp.float32,
            )
            for r in range(CAP):
                for half in range(blocks):
                    spread[r * COMPS + comp, pl.ds(i * blocks + half, DEVICES, stride=8), :] = (
                        moved[
                            r * DEVICES : (r + 1) * DEVICES, half * LANES : (half + 1) * LANES
                        ]
                    )
        return 0

    lax.fori_loop(0, SIDE, step, 0)
    part = DEVICES // 8

    def pack(i, _):
        for row in range(CAP * COMPS):
            message[pl.ds(i * part, part), pl.ds(row * 8, 8), :] = (
                spread[row, pl.ds(pl.multiple_of(i * part * 8, part * 8), part * 8), :]
                .reshape(part, 8, LANES)
                .astype(jnp.bfloat16)
            )
        return 0

    lax.fori_loop(0, 8, pack, 0)


def build(lines, pieces, high, low, picks):
    rows, wide = lines[0].shape[1:]
    points = picks.shape[1]
    remote = pl.BlockSpec(memory_space=pltpu.HBM)
    whole = pl.BlockSpec(memory_space=pltpu.VMEM)
    sent = (DEVICES, CAP * COMPS * 8, LANES)
    return pl.pallas_call(
        functools.partial(build_kernel, points, rows),
        out_shape=jax.ShapeDtypeStruct(sent, jnp.bfloat16),
        in_specs=[remote] * 3 + [whole] * 6 + [remote],
        out_specs=whole,
        scratch_shapes=[
            pltpu.VMEM((SIDE, 8, rows, wide), jnp.bfloat16),
            pltpu.VMEM(picks.shape, jnp.bfloat16),
            pltpu.VMEM((8 * rows, wide), jnp.bfloat16),
            pltpu.VMEM((CAP * COMPS, DEVICES * 8, LANES), jnp.float32),
            pltpu.SemaphoreType.DMA((4,)),
        ],
        compiler_params=pltpu.CompilerParams(vmem_limit_bytes=20 << 20),
        name="build",
    )(*lines, *pieces, high, low, picks)


def settle_kernel(count, received, out, wide, narrow, ready, out_sems):
    parts = DEVICES // count
    planes = count // (2 * SIDE)

    def lines(i):
        return pl.ds(pl.multiple_of(i * count * CAP, count * CAP), count * CAP)

    def leave(i):
        return pltpu.make_async_copy(ready.at[:, lines(i)], out.at[:, lines(i)], out_sems.at[i])

    def step(i, _):
        for core in range(2):
            for plane in range(planes):
                y, z = (i * planes + plane) // SIDE, lax.rem(i * planes + plane, SIDE)
                run = received[pl.ds(position(y, z, 0, core), SIDE)]
                wide[pl.ds((core * planes + plane) * SIDE * 72, SIDE * 72), :] = run.reshape(
                    SIDE * 72, LANES
                ).astype(jnp.float32)
        for comp in range(COMPS):
            for j in range(8):
                for r in range(CAP):
                    for core in range(2):
                        narrow[
                            comp * 8 + j, pl.ds(core * CAP + r, count // 2, stride=2 * CAP), :
                        ] = wide[
                            pl.ds(
                                core * count // 2 * 72 + (r * COMPS + comp) * 8 + j,
                                count // 2,
                                stride=72,
                            ),
                            :,
                        ]
        for comp in range(COMPS):
            for j in range(8):
                ready[comp, lines(i), j * LANES : (j + 1) * LANES] = narrow[comp * 8 + j].astype(
                    jnp.bfloat16
                )
        leave(i).start()
        return 0

    lax.fori_loop(0, parts, step, 0)
    for i in range(parts):
        leave(i).wait()


def settle(received):
    count = 16
    shape = (COMPS, DEVICES * CAP, 8 * LANES)
    return pl.pallas_call(
        functools.partial(settle_kernel, count),
        out_shape=jax.ShapeDtypeStruct(shape, jnp.bfloat16),
        in_specs=[pl.BlockSpec(memory_space=pltpu.VMEM)],
        out_specs=pl.BlockSpec(memory_space=pl.ANY),
        scratch_shapes=[
            pltpu.VMEM((count * 72, LANES), jnp.float32),
            pltpu.VMEM((COMPS * 8, count * CAP, LANES), jnp.float32),
            pltpu.VMEM(shape, jnp.bfloat16),
            pltpu.SemaphoreType.DMA((DEVICES // count,)),
        ],
        compiler_params=pltpu.CompilerParams(vmem_limit_bytes=9 << 20),
        name="settle",
    )(received)


def steps(coeffs, basis, route):
    points = basis.shape[1]
    high, low, picks = prepare(route.reshape(1, -1), jnp.transpose(basis[0], (1, 0, 2)))
    own = coeffs[0]
    near = [own]
    for k in range(1, SIDE):
        near.append(turn(own, "z", "x", k))
    line = lax.optimization_barrier(jnp.stack(near))
    mate = partner(line)

    def far(array, first, second, k):
        moved = turn(array, first, second, k)
        return moved, partner(moved)

    lines = []
    lines.append(expand(line, mate, high, low, points))
    for k in (1, 3):
        moved, swapped = far(line, "x", "z", k)
        lines.append(expand(moved, swapped, high, low, points))
    a, a_swapped = far(line[:2], "x", "z", 2)
    b, b_swapped = far(mate[2:], "z", "x", 2)
    message = build(lines, (a, b_swapped, a_swapped, b), high, low, picks)
    received = lax.all_to_all(message, ("c", "z", "y", "x"), split_axis=0, concat_axis=0, tiled=True)
    return jnp.transpose(settle(received), (1, 0, 2))


def solution(mesh):
    fine = Mesh(mesh.devices.reshape(SIDE, SIDE, SIDE, 2), ("y", "z", "x", "c"))
    row = ("z", "x", "c")
    everyone = ("y",) + row
    in_specs = (P("y", row, None), P("y", row, None, None), P(everyone, None))
    out_specs = P(everyone, None, None)
    return jax.shard_map(steps, mesh=fine, in_specs=in_specs, out_specs=out_specs, check_vma=False)
```

```python
import functools

import jax
import jax.numpy as jnp
from jax import lax
from jax.experimental import pallas as pl
from jax.experimental.pallas import tpu as pltpu
from jax.sharding import Mesh
from jax.sharding import PartitionSpec as P


SIDE = 4
DEVICES = 128
CAP = 3
COMPS = 3
LANES = 128


def place(z, x, c):
    return (z * SIDE + x) * 2 + c


def position(y, z, x, c):
    return ((c * SIDE + z) * SIDE + y) * SIDE + x


def device_at(slot):
    y, z, x, c = (slot >> 2) & 3, (slot >> 4) & 3, slot & 3, slot >> 6
    return ((y * SIDE + z) * SIDE + x) * 2 + c


def turn(array, first, second, k):
    pairs = []
    for z in range(SIDE):
        for x in range(SIDE):
            for c in range(2):
                axis = (first, second)[c]
                tz = (z + k) % SIDE if axis == "z" else z
                tx = (x + k) % SIDE if axis == "x" else x
                pairs.append((place(z, x, c), place(tz, tx, c)))
    return lax.ppermute(array, ("z", "x", "c"), pairs)


def partner(array):
    return lax.ppermute(array, ("z", "x", "c"), [(i, i ^ 1) for i in range(2 * SIDE * SIDE)])


def split(value):
    high = value.astype(jnp.bfloat16)
    return high, (value - high.astype(jnp.float32)).astype(jnp.bfloat16)


def prepare_kernel(points, route, basis, high, low, picks_out, base, picks, sems, sem):
    copies = [
        pltpu.make_async_copy(basis.at[comp], base.at[comp], sems.at[comp]) for comp in range(COMPS)
    ]
    for copy in copies:
        copy.start()
    mine = device_at(lax.broadcasted_iota(jnp.int32, (DEVICES, points), 0)) == route[...]
    before = lax.broadcasted_iota(jnp.int32, (points, points), 0) < lax.broadcasted_iota(
        jnp.int32, (points, points), 1
    )
    count = jnp.dot(
        jnp.where(mine, 1.0, 0.0).astype(jnp.bfloat16),
        jnp.where(before, 1.0, 0.0).astype(jnp.bfloat16),
        preferred_element_type=jnp.float32,
    )
    for r in range(CAP):
        picks[pl.ds(r * DEVICES, DEVICES), :] = jnp.where(
            mine & (count == float(r)), 1.0, 0.0
        ).astype(jnp.bfloat16)
    copy = pltpu.make_async_copy(picks, picks_out, sem)
    copy.start()
    for comp in range(COMPS):
        copies[comp].wait()
        high[pl.ds(comp * points, points), :], low[pl.ds(comp * points, points), :] = split(
            base[comp]
        )
    copy.wait()


def prepare(route, basis):
    comps, points, modes = basis.shape
    whole = pl.BlockSpec(memory_space=pltpu.VMEM)
    half = jax.ShapeDtypeStruct((comps * points, modes), jnp.bfloat16)
    return pl.pallas_call(
        functools.partial(prepare_kernel, points),
        out_shape=(half, half, jax.ShapeDtypeStruct((CAP * DEVICES, points), jnp.bfloat16)),
        in_specs=[whole, pl.BlockSpec(memory_space=pltpu.HBM)],
        out_specs=(whole, whole, pl.BlockSpec(memory_space=pltpu.HBM)),
        scratch_shapes=[
            pltpu.VMEM((comps, points, modes), jnp.float32),
            pltpu.VMEM((CAP * DEVICES, points), jnp.bfloat16),
            pltpu.SemaphoreType.DMA((comps,)),
            pltpu.SemaphoreType.DMA,
        ],
        compiler_params=pltpu.CompilerParams(vmem_limit_bytes=52_000_000),
        cost_estimate=pl.CostEstimate(flops=20_000_000, bytes_accessed=8 << 20, transcendentals=0),
        name="prepare",
    )(route, basis)


def product(points, coef, high, low, result):
    contract = functools.partial(
        lax.dot_general,
        dimension_numbers=(((1,), (1,)), ((), ())),
        preferred_element_type=jnp.float32,
    )
    top, rest = split(coef)
    for comp in range(COMPS):
        there = pl.ds(comp * points, points)
        value = contract(rest, high[there, :])
        value = value + contract(top, low[there, :])
        value = value + contract(top, high[there, :])
        value = value.astype(jnp.bfloat16)
        result[:, :, comp * points : (comp + 1) * points] = value.reshape(
            result.shape[:2] + (points,)
        )


def gathered(pieces):
    modes = pieces[0].shape[-1]
    return jnp.concatenate([piece[...].reshape(-1, modes) for piece in pieces], axis=0)


def expand_kernel(points, high, low, mine, mate, out, result, sem):
    product(points, gathered((mine, mate)), high, low, result)
    copy = pltpu.make_async_copy(result, out, sem)
    copy.start()
    copy.wait()


def expand(mine, mate, high, low, points):
    rows = mine.shape[1]
    shape = (8, rows, COMPS * points)
    return pl.pallas_call(
        functools.partial(expand_kernel, points),
        out_shape=jax.ShapeDtypeStruct(shape, jnp.bfloat16),
        in_specs=[pl.BlockSpec(memory_space=pltpu.VMEM)] * 4,
        out_specs=pl.BlockSpec(memory_space=pltpu.HBM),
        scratch_shapes=[pltpu.VMEM(shape, jnp.bfloat16), pltpu.SemaphoreType.DMA],
        compiler_params=pltpu.CompilerParams(vmem_limit_bytes=10 << 20),
        cost_estimate=pl.CostEstimate(
            flops=1_200_000_000, bytes_accessed=1 << 20, transcendentals=0
        ),
        name="expand",
    )(high, low, mine, mate)


def build_kernel(points, rows, *refs):
    lines, pieces = refs[:3], refs[3:5]
    high, low, picks_in, message = refs[5:9]
    table, picks, spread, in_sems = refs[9:]
    z, x, c = lax.axis_index("z"), lax.axis_index("x"), lax.axis_index("c")
    copies = [
        pltpu.make_async_copy(line, table.at[k], in_sems.at[i])
        for i, (line, k) in enumerate(zip(lines, (0, 1, 3)))
    ]
    copies.append(pltpu.make_async_copy(picks_in, picks, in_sems.at[3]))
    for copy in copies:
        copy.start()
    product(points, gathered(pieces), high, low, table.at[2])
    for copy in copies:
        copy.wait()

    width = 8 * rows
    blocks = width // LANES

    def step(i, _):
        dz = lax.rem(z - i + SIDE, SIDE)
        found = []
        for column in range(SIDE):
            dx = lax.rem(x - column + SIDE, SIDE)
            for core in range(2):
                k, inner = (dx, dz) if core == 0 else (dz, dx)
                side = jnp.where(c == core, 0, SIDE)
                found.append(table[k, side + inner])
        chunk = jnp.concatenate(found, axis=0)
        for comp in range(COMPS):
            moved = lax.dot_general(
                picks[...],
                chunk[:, comp * points : (comp + 1) * points],
                (((1,), (1,)), ((), ())),
                preferred_element_type=jnp.float32,
            )
            for r in range(CAP):
                for half in range(blocks):
                    spread[r * COMPS + comp, pl.ds(i * blocks + half, DEVICES, stride=8), :] = (
                        moved[
                            r * DEVICES : (r + 1) * DEVICES, half * LANES : (half + 1) * LANES
                        ]
                    )
        return 0

    lax.fori_loop(0, SIDE, step, 0)
    part = DEVICES // 8

    def pack(i, _):
        for row in range(CAP * COMPS):
            message[pl.ds(i * part, part), pl.ds(row * 8, 8), :] = (
                spread[row, pl.ds(pl.multiple_of(i * part * 8, part * 8), part * 8), :]
                .reshape(part, 8, LANES)
                .astype(jnp.bfloat16)
            )
        return 0

    lax.fori_loop(0, 8, pack, 0)


def build(lines, pieces, high, low, picks):
    rows, wide = lines[0].shape[1:]
    points = picks.shape[1]
    remote = pl.BlockSpec(memory_space=pltpu.HBM)
    whole = pl.BlockSpec(memory_space=pltpu.VMEM)
    sent = (DEVICES, CAP * COMPS * 8, LANES)
    return pl.pallas_call(
        functools.partial(build_kernel, points, rows),
        out_shape=jax.ShapeDtypeStruct(sent, jnp.bfloat16),
        in_specs=[remote] * 3 + [whole] * 4 + [remote],
        out_specs=whole,
        scratch_shapes=[
            pltpu.VMEM((SIDE, 8, rows, wide), jnp.bfloat16),
            pltpu.VMEM(picks.shape, jnp.bfloat16),
            pltpu.VMEM((CAP * COMPS, DEVICES * 8, LANES), jnp.float32),
            pltpu.SemaphoreType.DMA((4,)),
        ],
        compiler_params=pltpu.CompilerParams(vmem_limit_bytes=20 << 20),
        name="build",
    )(*lines, *pieces, high, low, picks)


def settle_kernel(count, received, out, wides, narrows, ready, out_sems):
    parts = DEVICES // count
    planes = count // (2 * SIDE)

    def lines(i):
        return pl.ds(i * count * CAP, count * CAP)

    def leave(i):
        return pltpu.make_async_copy(ready.at[:, lines(i)], out.at[:, lines(i)], out_sems.at[i])

    def step(i):
        for core in range(2):
            for plane in range(planes):
                y, z = divmod(i * planes + plane, SIDE)
                run = received[pl.ds(position(y, z, 0, core), SIDE)]
                wides[i % 2, pl.ds((core * planes + plane) * SIDE * 72, SIDE * 72), :] = run.reshape(
                    SIDE * 72, LANES
                ).astype(jnp.float32)
        for comp in range(COMPS):
            for j in range(8):
                for r in range(CAP):
                    for core in range(2):
                        narrows[
                            i % 2, comp * 8 + j, pl.ds(core * CAP + r, count // 2, stride=2 * CAP), :
                        ] = wides[
                            i % 2,
                            pl.ds(
                                core * count // 2 * 72 + (r * COMPS + comp) * 8 + j,
                                count // 2,
                                stride=72,
                            ),
                            :,
                        ]
        for comp in range(COMPS):
            for j in range(8):
                ready[comp, lines(i), j * LANES : (j + 1) * LANES] = narrows[i % 2, comp * 8 + j].astype(
                    jnp.bfloat16
                )
        leave(i).start()
        return 0

    for i in range(parts):
        step(i)
    for i in range(parts):
        leave(i).wait()


def settle(received):
    count = 16
    shape = (COMPS, DEVICES * CAP, 8 * LANES)
    return pl.pallas_call(
        functools.partial(settle_kernel, count),
        out_shape=jax.ShapeDtypeStruct(shape, jnp.bfloat16),
        in_specs=[pl.BlockSpec(memory_space=pltpu.VMEM)],
        out_specs=pl.BlockSpec(memory_space=pl.ANY),
        scratch_shapes=[
            pltpu.VMEM((2, count * 72, LANES), jnp.float32),
            pltpu.VMEM((2, COMPS * 8, count * CAP, LANES), jnp.float32),
            pltpu.VMEM(shape, jnp.bfloat16),
            pltpu.SemaphoreType.DMA((DEVICES // count,)),
        ],
        compiler_params=pltpu.CompilerParams(vmem_limit_bytes=9 << 20),
        name="settle",
    )(received)


def steps(coeffs, basis, route):
    points = basis.shape[1]
    high, low, picks = prepare(route.reshape(1, -1), jnp.transpose(basis[0], (1, 0, 2)))
    own = coeffs[0]
    near = [own]
    for k in range(1, SIDE):
        near.append(turn(own, "z", "x", k))
    line = jnp.stack(near)
    mate = partner(line)

    def far(array, first, second, k):
        moved = turn(array, first, second, k)
        return moved, partner(moved)

    lines = []
    lines.append(expand(line, mate, high, low, points))
    for k in (1, 3):
        moved, swapped = far(line, "x", "z", k)
        lines.append(expand(moved, swapped, high, low, points))
    message = build(lines, far(line, "x", "z", 2), high, low, picks)
    received = lax.all_to_all(message, ("c", "z", "y", "x"), split_axis=0, concat_axis=0, tiled=True)
    return jnp.transpose(settle(received), (1, 0, 2))


def solution(mesh):
    fine = Mesh(mesh.devices.reshape(SIDE, SIDE, SIDE, 2), ("y", "z", "x", "c"))
    row = ("z", "x", "c")
    everyone = ("y",) + row
    in_specs = (P("y", row, None), P("y", row, None, None), P(everyone, None))
    out_specs = P(everyone, None, None)
    return jax.shard_map(steps, mesh=fine, in_specs=in_specs, out_specs=out_specs, check_vma=False)
```

```python
import functools

import jax
import jax.numpy as jnp
from jax import lax
from jax.experimental import pallas as pl
from jax.experimental.pallas import tpu as pltpu
from jax.sharding import Mesh
from jax.sharding import PartitionSpec as P


SIDE = 4
DEVICES = 128
CAP = 3
COMPS = 3
LANES = 128


def place(z, x, c):
    return (z * SIDE + x) * 2 + c


def position(y, z, x, c):
    return ((c * SIDE + z) * SIDE + y) * SIDE + x


def device_at(slot):
    y, z, x, c = (slot >> 2) & 3, (slot >> 4) & 3, slot & 3, slot >> 6
    return ((y * SIDE + z) * SIDE + x) * 2 + c


def turn(array, first, second, k):
    pairs = []
    for z in range(SIDE):
        for x in range(SIDE):
            for c in range(2):
                axis = (first, second)[c]
                tz = (z + k) % SIDE if axis == "z" else z
                tx = (x + k) % SIDE if axis == "x" else x
                pairs.append((place(z, x, c), place(tz, tx, c)))
    return lax.ppermute(array, ("z", "x", "c"), pairs)


def partner(array):
    return lax.ppermute(array, ("z", "x", "c"), [(i, i ^ 1) for i in range(2 * SIDE * SIDE)])


def split(value):
    high = value.astype(jnp.bfloat16)
    return high, (value - high.astype(jnp.float32)).astype(jnp.bfloat16)


def prepare_kernel(points, route, basis, high, low, picks_out, base, picks, sems, sem):
    copies = [
        pltpu.make_async_copy(basis.at[comp], base.at[comp], sems.at[comp]) for comp in range(COMPS)
    ]
    for copy in copies:
        copy.start()
    mine = device_at(lax.broadcasted_iota(jnp.int32, (DEVICES, points), 0)) == route[...]
    before = lax.broadcasted_iota(jnp.int32, (points, points), 0) < lax.broadcasted_iota(
        jnp.int32, (points, points), 1
    )
    count = jnp.dot(
        jnp.where(mine, 1.0, 0.0).astype(jnp.bfloat16),
        jnp.where(before, 1.0, 0.0).astype(jnp.bfloat16),
        preferred_element_type=jnp.float32,
    )
    for r in range(CAP):
        picks[pl.ds(r * DEVICES, DEVICES), :] = jnp.where(
            mine & (count == float(r)), 1.0, 0.0
        ).astype(jnp.bfloat16)
    copy = pltpu.make_async_copy(picks, picks_out, sem)
    copy.start()
    for comp in range(COMPS):
        copies[comp].wait()
        high[pl.ds(comp * points, points), :], low[pl.ds(comp * points, points), :] = split(
            base[comp]
        )
    copy.wait()


def prepare(route, basis):
    comps, points, modes = basis.shape
    whole = pl.BlockSpec(memory_space=pltpu.VMEM)
    half = jax.ShapeDtypeStruct((comps * points, modes), jnp.bfloat16)
    return pl.pallas_call(
        functools.partial(prepare_kernel, points),
        out_shape=(half, half, jax.ShapeDtypeStruct((CAP * DEVICES, points), jnp.bfloat16)),
        in_specs=[whole, pl.BlockSpec(memory_space=pltpu.HBM)],
        out_specs=(whole, whole, pl.BlockSpec(memory_space=pltpu.HBM)),
        scratch_shapes=[
            pltpu.VMEM((comps, points, modes), jnp.float32),
            pltpu.VMEM((CAP * DEVICES, points), jnp.bfloat16),
            pltpu.SemaphoreType.DMA((comps,)),
            pltpu.SemaphoreType.DMA,
        ],
        compiler_params=pltpu.CompilerParams(vmem_limit_bytes=52_000_000),
        cost_estimate=pl.CostEstimate(flops=20_000_000, bytes_accessed=8 << 20, transcendentals=0),
        name="prepare",
    )(route, basis)


def product(points, coef, high, low, result):
    contract = functools.partial(
        lax.dot_general,
        dimension_numbers=(((1,), (1,)), ((), ())),
        preferred_element_type=jnp.float32,
    )
    top, rest = split(coef)
    for comp in range(COMPS):
        there = pl.ds(comp * points, points)
        value = contract(rest, high[there, :])
        value = value + contract(top, low[there, :])
        value = value + contract(top, high[there, :])
        value = value.astype(jnp.bfloat16)
        result[:, :, comp * points : (comp + 1) * points] = value.reshape(
            result.shape[:2] + (points,)
        )


def gathered(pieces):
    modes = pieces[0].shape[-1]
    return jnp.concatenate([piece[...].reshape(-1, modes) for piece in pieces], axis=0)


def expand_kernel(points, high, low, mine, mate, out, result, sem):
    product(points, gathered((mine, mate)), high, low, result)
    copy = pltpu.make_async_copy(result, out, sem)
    copy.start()
    copy.wait()


def expand(mine, mate, high, low, points):
    rows = mine.shape[1]
    shape = (8, rows, COMPS * points)
    return pl.pallas_call(
        functools.partial(expand_kernel, points),
        out_shape=jax.ShapeDtypeStruct(shape, jnp.bfloat16),
        in_specs=[pl.BlockSpec(memory_space=pltpu.VMEM)] * 4,
        out_specs=pl.BlockSpec(memory_space=pltpu.HBM),
        scratch_shapes=[pltpu.VMEM(shape, jnp.bfloat16), pltpu.SemaphoreType.DMA],
        compiler_params=pltpu.CompilerParams(vmem_limit_bytes=10 << 20),
        cost_estimate=pl.CostEstimate(
            flops=1_200_000_000, bytes_accessed=1 << 20, transcendentals=0
        ),
        name="expand",
    )(high, low, mine, mate)


def build_kernel(points, rows, *refs):
    lines, pieces = refs[:3], refs[3:5]
    high, low, picks_in, message = refs[5:9]
    table, picks, spread, in_sems = refs[9:]
    z, x, c = lax.axis_index("z"), lax.axis_index("x"), lax.axis_index("c")
    copies = [
        pltpu.make_async_copy(line, table.at[k], in_sems.at[i])
        for i, (line, k) in enumerate(zip(lines, (0, 1, 2)))
    ]
    copies.append(pltpu.make_async_copy(picks_in, picks, in_sems.at[3]))
    for copy in copies:
        copy.start()
    product(points, gathered(pieces), high, low, table.at[3])
    for copy in copies:
        copy.wait()

    width = 8 * rows
    blocks = width // LANES

    def step(i, _):
        dz = lax.rem(z - i + SIDE, SIDE)
        found = []
        for column in range(SIDE):
            dx = lax.rem(x - column + SIDE, SIDE)
            for core in range(2):
                k, inner = (dx, dz) if core == 0 else (dz, dx)
                side = jnp.where(c == core, 0, SIDE)
                found.append(table[k, side + inner])
        chunk = jnp.concatenate(found, axis=0)
        for comp in range(COMPS):
            moved = lax.dot_general(
                picks[...],
                chunk[:, comp * points : (comp + 1) * points],
                (((1,), (1,)), ((), ())),
                preferred_element_type=jnp.float32,
            )
            for r in range(CAP):
                for half in range(blocks):
                    spread[r * COMPS + comp, pl.ds(i * blocks + half, DEVICES, stride=8), :] = (
                        moved[
                            r * DEVICES : (r + 1) * DEVICES, half * LANES : (half + 1) * LANES
                        ]
                    )
        return 0

    lax.fori_loop(0, SIDE, step, 0)
    part = DEVICES // 8

    def pack(i, _):
        for row in range(CAP * COMPS):
            message[pl.ds(i * part, part), pl.ds(row * 8, 8), :] = (
                spread[row, pl.ds(pl.multiple_of(i * part * 8, part * 8), part * 8), :]
                .reshape(part, 8, LANES)
                .astype(jnp.bfloat16)
            )
        return 0

    lax.fori_loop(0, 8, pack, 0)


def build(lines, pieces, high, low, picks):
    rows, wide = lines[0].shape[1:]
    points = picks.shape[1]
    remote = pl.BlockSpec(memory_space=pltpu.HBM)
    whole = pl.BlockSpec(memory_space=pltpu.VMEM)
    sent = (DEVICES, CAP * COMPS * 8, LANES)
    return pl.pallas_call(
        functools.partial(build_kernel, points, rows),
        out_shape=jax.ShapeDtypeStruct(sent, jnp.bfloat16),
        in_specs=[remote] * 3 + [whole] * 4 + [remote],
        out_specs=whole,
        scratch_shapes=[
            pltpu.VMEM((SIDE, 8, rows, wide), jnp.bfloat16),
            pltpu.VMEM(picks.shape, jnp.bfloat16),
            pltpu.VMEM((CAP * COMPS, DEVICES * 8, LANES), jnp.float32),
            pltpu.SemaphoreType.DMA((4,)),
        ],
        compiler_params=pltpu.CompilerParams(vmem_limit_bytes=20 << 20),
        name="build",
    )(*lines, *pieces, high, low, picks)


def settle_kernel(count, received, out, wides, narrows, ready, out_sems):
    parts = DEVICES // count
    planes = count // (2 * SIDE)

    def lines(i):
        return pl.ds(i * count * CAP, count * CAP)

    def leave(i):
        return pltpu.make_async_copy(ready.at[:, lines(i)], out.at[:, lines(i)], out_sems.at[i])

    def step(i):
        for core in range(2):
            for plane in range(planes):
                y, z = divmod(i * planes + plane, SIDE)
                run = received[pl.ds(position(y, z, 0, core), SIDE)]
                wides[i % 2, pl.ds((core * planes + plane) * SIDE * 72, SIDE * 72), :] = run.reshape(
                    SIDE * 72, LANES
                ).astype(jnp.float32)
        for comp in range(COMPS):
            for j in range(8):
                for r in range(CAP):
                    for core in range(2):
                        narrows[
                            i % 2, comp * 8 + j, pl.ds(core * CAP + r, count // 2, stride=2 * CAP), :
                        ] = wides[
                            i % 2,
                            pl.ds(
                                core * count // 2 * 72 + (r * COMPS + comp) * 8 + j,
                                count // 2,
                                stride=72,
                            ),
                            :,
                        ]
        for comp in range(COMPS):
            for j in range(8):
                ready[comp, lines(i), j * LANES : (j + 1) * LANES] = narrows[i % 2, comp * 8 + j].astype(
                    jnp.bfloat16
                )
        leave(i).start()
        return 0

    for i in range(parts):
        step(i)
    for i in range(parts):
        leave(i).wait()


def settle(received):
    count = 16
    shape = (COMPS, DEVICES * CAP, 8 * LANES)
    return pl.pallas_call(
        functools.partial(settle_kernel, count),
        out_shape=jax.ShapeDtypeStruct(shape, jnp.bfloat16),
        in_specs=[pl.BlockSpec(memory_space=pltpu.VMEM)],
        out_specs=pl.BlockSpec(memory_space=pl.ANY),
        scratch_shapes=[
            pltpu.VMEM((2, count * 72, LANES), jnp.float32),
            pltpu.VMEM((2, COMPS * 8, count * CAP, LANES), jnp.float32),
            pltpu.VMEM(shape, jnp.bfloat16),
            pltpu.SemaphoreType.DMA((DEVICES // count,)),
        ],
        compiler_params=pltpu.CompilerParams(vmem_limit_bytes=9 << 20),
        name="settle",
    )(received)


def steps(coeffs, basis, route):
    points = basis.shape[1]
    high, low, picks = prepare(route.reshape(1, -1), jnp.transpose(basis[0], (1, 0, 2)))
    own = coeffs[0]
    near = [own]
    for k in range(1, SIDE):
        near.append(turn(own, "z", "x", k))
    line = jnp.stack(near)
    mate = partner(line)

    def far(array, first, second, k):
        moved = turn(array, first, second, k)
        return moved, partner(moved)

    lines = []
    lines.append(expand(line, mate, high, low, points))
    for k in (1, 2):
        moved, swapped = far(line, "x", "z", k)
        lines.append(expand(moved, swapped, high, low, points))
    message = build(lines, far(line, "x", "z", 3), high, low, picks)
    received = lax.all_to_all(message, ("c", "z", "y", "x"), split_axis=0, concat_axis=0, tiled=True)
    return jnp.transpose(settle(received), (1, 0, 2))


def solution(mesh):
    fine = Mesh(mesh.devices.reshape(SIDE, SIDE, SIDE, 2), ("y", "z", "x", "c"))
    row = ("z", "x", "c")
    everyone = ("y",) + row
    in_specs = (P("y", row, None), P("y", row, None, None), P(everyone, None))
    out_specs = P(everyone, None, None)
    return jax.shard_map(steps, mesh=fine, in_specs=in_specs, out_specs=out_specs, check_vma=False)
```
